256 devices in a mesh: seq: 32 (over y_lo, z, core), tp: 8 (over x, y_hi).
Axes of the slice: x: 4, y: 4 (y_hi: 2, y_lo: 2; y = y_hi * 2 + y_lo), z: 8, core: 2. Of those that a mesh axis runs over, the one named last changes fastest.
Arguments:
- hidden: bfloat16 [8192, 4096], P('seq', 'tp'), may hold values from -6 to 6
- neighbours: bfloat16 [128, 256, 896], P('seq'), may hold values from -6 to 6
- enc_gain: float32 [896], replicated, may hold values from 0.25 to 1.75
- enc_w1: bfloat16 [896, 3584], P(None, 'tp'), may hold values from -0.1875 to 0.1875
- enc_w2: bfloat16 [3584, 896], P('tp'), may hold values from -0.09375 to 0.09375
- key_weight: bfloat16 [896, 4096], P(None, 'tp'), may hold values from -0.1875 to 0.1875
- value_weight: bfloat16 [896, 4096], P(None, 'tp'), may hold values from -0.1875 to 0.1875
- dec_gain: float32 [4096], replicated, may hold values from 0.25 to 1.75
- query_weight: bfloat16 [4096, 4096], P('seq', 'tp'), may hold values from -0.09375 to 0.09375
- out_weight: bfloat16 [4096, 4096], P('tp', 'seq'), may hold values from -0.09375 to 0.09375
Outputs:
- mixed: bfloat16 [8192, 4096], P('seq', 'tp')
The draws below stay inside these ranges and needn't reach their ends.
All inputs are finite; a program needn't handle non-finite values.
Results may differ from the reference program's by a relative error of at most 0.015.
Values may be sent and summed in bfloat16 or wider, within the bound.
A program may use at most 64 MiB of HBM per device.

```python
import jax
import jax.numpy as jnp
from jax import lax

D = 4096
HEADS = 32
HD = 128
E = 896
EFF = 3584
M = 64
NEIGH = 2
RLEN = 128
TOKENS = 8192
SPANS = 128
N_TP = 8


def shard_levels(key, shape, cuts, low, high):
    def one(axis_at, shards_of):
        steps = jax.random.uniform(jax.random.fold_in(jax.random.fold_in(key, 6), axis_at), (shards_of,), jnp.float32, low / len(cuts), high / len(cuts))
        return jnp.repeat(jnp.exp(steps), shape[axis_at] // shards_of).reshape((-1,) + (1,) * (len(shape) - axis_at - 1))

    factor_of = one(*cuts[0])
    for cut in cuts[1:]:
        factor_of = factor_of * one(*cut)
    return factor_of


def normal_values(rng, extent, deviation, limit, pieces=(), held_as=jnp.bfloat16):
    result = deviation * jax.random.normal(rng, extent, jnp.float32)
    if pieces:
        result = result * shard_levels(rng, extent, pieces, -0.22, 0.18)
    return jnp.clip(result, -limit, limit).astype(held_as)


def setup_inputs(seed: int = 0) -> dict:
    streams_of = jax.random.split(jax.random.key(seed), 11)
    return {
        "hidden": normal_values(streams_of[0], (TOKENS, D), 1.0, 6.0, ((0, 32), (1, 8))),
        "neighbours": normal_values(streams_of[1], (SPANS, NEIGH * RLEN, E), 1.0, 6.0, ((0, 32),)),
        "enc_gain": jnp.clip(1.0 + 0.15 * jax.random.normal(streams_of[2], (E,), jnp.float32), 0.25, 1.75),
        "enc_w1": normal_values(streams_of[3], (E, EFF), E ** -0.5, 0.1875, ((1, 8),)),
        "enc_w2": normal_values(streams_of[4], (EFF, E), EFF ** -0.5, 0.09375, ((0, 8),)),
        "key_weight": normal_values(streams_of[5], (E, HEADS * HD), E ** -0.5, 0.1875, ((1, 8),)),
        "value_weight": normal_values(streams_of[6], (E, HEADS * HD), E ** -0.5, 0.1875, ((1, 8),)),
        "dec_gain": jnp.clip(1.0 + 0.15 * jax.random.normal(streams_of[7], (D,), jnp.float32), 0.25, 1.75),
        "query_weight": normal_values(streams_of[8], (D, HEADS * HD), D ** -0.5, 0.09375, ((0, 32), (1, 8))),
        "out_weight": normal_values(streams_of[9], (HEADS * HD, D), (HEADS * HD) ** -0.5, 0.09375, ((0, 8), (1, 32))),
    }


def rms_scale(values32, gain):
    return values32 * lax.rsqrt(lax.optimization_barrier(jnp.mean(values32 * values32, axis=-1, keepdims=True)) + 1e-06) * gain.astype(jnp.float32)

def reference(hidden, neighbours, enc_gain, enc_w1, enc_w2, key_weight, value_weight, dec_gain, query_weight, out_weight):
    hidden32 = hidden.astype(jnp.float32)
    dec_norm = rms_scale(hidden32, dec_gain).astype(jnp.bfloat16)
    query = jnp.dot(dec_norm, query_weight, preferred_element_type=jnp.float32).astype(jnp.bfloat16)
    flat = neighbours.reshape(SPANS * NEIGH * RLEN, E)
    enc_norm = rms_scale(flat.astype(jnp.float32), enc_gain).astype(jnp.bfloat16)
    inner = jax.nn.relu(jnp.dot(enc_norm, enc_w1, preferred_element_type=jnp.float32)).astype(jnp.bfloat16)
    encoded = (flat.astype(jnp.float32) + jnp.dot(inner, enc_w2, preferred_element_type=jnp.float32)).astype(jnp.bfloat16)
    keys = jnp.dot(encoded, key_weight, preferred_element_type=jnp.float32).astype(jnp.bfloat16)
    values = jnp.dot(encoded, value_weight, preferred_element_type=jnp.float32).astype(jnp.bfloat16)
    keys = keys.reshape(SPANS, NEIGH * RLEN, HEADS, HD)
    values = values.reshape(SPANS, NEIGH * RLEN, HEADS, HD)
    blank = jnp.zeros((1, NEIGH * RLEN, HEADS, HD), jnp.bfloat16)
    keys = jnp.concatenate([blank, keys], axis=0)
    values = jnp.concatenate([blank, values], axis=0)
    grouped = jnp.pad(query, ((1, M - 1), (0, 0))).reshape(SPANS + 1, M, HEADS, HD)
    scores = jnp.einsum('cmhd,cnhd->chmn', grouped.astype(jnp.float32), keys.astype(jnp.float32)) * HD ** (-0.5)
    probs = jax.nn.softmax(scores, axis=-1).astype(jnp.bfloat16)
    attn = jnp.einsum('chmn,cnhd->cmhd', probs.astype(jnp.float32), values.astype(jnp.float32)).astype(jnp.bfloat16)
    attn = attn.reshape((SPANS + 1) * M, HEADS * HD)[1:TOKENS + 1]
    position = jnp.arange(TOKENS, dtype=jnp.int32)[:, None]
    attn = jnp.where(position >= M - 1, attn, jnp.zeros_like(attn))
    group_width = HEADS * HD // N_TP
    branch = jnp.zeros((TOKENS, D), jnp.float32)
    for group in range(N_TP):
        lower = group * group_width
        partial_value = jnp.dot(attn[:, lower:lower + group_width], out_weight[lower:lower + group_width], preferred_element_type=jnp.float32).astype(jnp.bfloat16)
        partial_value = lax.optimization_barrier(partial_value)
        branch = branch + partial_value.astype(jnp.float32)
    return (hidden32 + branch).astype(jnp.bfloat16)
```

```python
import functools

import jax
import jax.numpy as jnp
from jax import lax
from jax.experimental import pallas as pl
from jax.experimental.pallas import tpu as pltpu
from jax.sharding import PartitionSpec as P

HD = 128
M = 64
BF = jnp.bfloat16
F32 = jnp.float32
MESH = pl.DeviceIdType.MESH

NX = 4
NZ = 8
ENC_A = 48
DEC_A = 96


def dot(a, b):
    return jnp.dot(a, b, preferred_element_type=F32)


def dot_t(a, b):
    return lax.dot_general(a, b, (((1,), (1,)), ((), ())), preferred_element_type=F32)


class Mover:
    def __init__(self, send, recv):
        self.send, self.recv = send, recv

    def copy(self, i, src, dst, device):
        return pltpu.make_async_remote_copy(
            src_ref=src,
            dst_ref=dst,
            send_sem=self.send.at[i],
            recv_sem=self.recv.at[i],
            device_id=device,
            device_id_type=MESH,
        )


def kernel(
    hid, nb, eg, w1, w2, wk, wv, dg, wq, wo, out,
    nbv, w1v, w2v, wkv, wvv, hbuf, wqb, wob,
    pbuf, ra, ryb, sb, rbx, sa, ray, ebuf,
    acc, qv, qn, qs, at, an, af,
    obuf, oa, oyb, osb, obx, osa, oay,
    lsem, hs, hr, es, er, rs, rr, bs, br, ws, wr, xs, xr,
):
    s = lax.axis_index("seq")
    t = lax.axis_index("tp")
    x, h = lax.div(t, 2), lax.rem(t, 2)
    yl, zc = lax.div(s, 16), lax.rem(s, 16)
    z, c = lax.div(zc, 2), lax.rem(zc, 2)
    nseq = lax.axis_size("seq")

    def at_x(k):
        return lax.rem(x + k, NX)

    def dev_x(k):
        return (s, at_x(k) * 2 + h)

    dev_h = (s, x * 2 + 1 - h)

    def at_z(k):
        return lax.rem(z + k + NZ, NZ)

    def dev_z(k):
        return (yl * 16 + at_z(k) * 2 + c, t)

    dev_c = (yl * 16 + z * 2 + 1 - c, t)
    dev_yl = ((1 - yl) * 16 + zc, t)
    dev_next = (lax.rem(s + 1, nseq), t)
    dev_prev = (lax.rem(s + nseq - 1, nseq), t)

    def local(i, src, dst):
        return pltpu.make_async_copy(src, dst, lsem.at[i])

    c_hid = local(0, hid, hbuf.at[x, h])
    c_wq = local(1, wq, wqb.at[yl, zc])
    c_w1 = local(2, w1, w1v)
    c_w2 = local(3, w2, w2v)
    c_wo = local(4, wo, wob.at[yl, zc])
    c_wk = local(5, wk, wkv)
    c_wv = local(6, wv, wvv)

    def c_nb(o):
        return local(7 + o, nb.at[at_x(o)], nbv.at[at_x(o)])

    c_hid.start()
    c_wq.start()
    c_nb(3).start()
    c_w1.start()
    c_w2.start()
    c_nb(2).start()
    c_nb(1).start()
    c_nb(0).start()
    c_wo.start()
    c_wk.start()
    c_wv.start()

    barrier = pltpu.get_barrier_semaphore()
    partners = [dev_x(1), dev_x(2), dev_x(3), dev_h, dev_z(1), dev_z(-1), dev_c, dev_yl, dev_next, dev_prev]
    for device in partners:
        pl.semaphore_signal(barrier, inc=1, device_id=device, device_id_type=MESH)
    pl.semaphore_wait(barrier, len(partners))

    started = []

    def go(cp):
        cp.start()
        started.append(cp)

    def ag_own(mv, buf, k):
        return mv.copy(k, buf.at[x, h], buf.at[x, h], dev_h if k == 0 else dev_x(k))

    def ag_own_in(mv, buf, k):
        ref = buf.at[x, 1 - h] if k == 0 else buf.at[at_x(NX - k), h]
        return mv.copy(k, ref, ref, dev_h)

    def ag_a(mv, buf, a, k):
        ref = buf.at[x, 1 - h, pl.ds(0, a)]
        return mv.copy(3 + k, ref, ref, dev_x(k))

    def ag_a_in(mv, buf, a, k):
        ref = buf.at[at_x(NX - k), 1 - h, pl.ds(0, a)]
        return mv.copy(3 + k, ref, ref, dev_h)

    def ag_b(mv, buf, a, k):
        rows = buf.shape[2]
        ref = buf.at[at_x(NX - k), h, pl.ds(a, rows - a)]
        return mv.copy(6 + k, ref, ref, dev_h)

    def ag_b_in(mv, buf, a, k):
        rows = buf.shape[2]
        ref = buf.at[at_x(NX - k), 1 - h, pl.ds(a, rows - a)]
        return mv.copy(6 + k, ref, ref, dev_h)

    hm, em = Mover(hs, hr), Mover(es, er)

    def ag_start(mv, buf):
        for k in (0, 1, 3, 2):
            go(ag_own(mv, buf, k))

    def ag_pass_a(mv, buf, a):
        ag_own_in(mv, buf, 0).wait_recv()
        for k in (1, 3, 2):
            go(ag_a(mv, buf, a, k))

    def ag_pass_b(mv, buf, a, k):
        ag_own_in(mv, buf, k).wait_recv()
        go(ag_b(mv, buf, a, k))

    def w_mover(i):
        return Mover(ws.at[i], wr.at[i])

    def blk(buf, cls, zz):
        return buf.at[cls, zz * 2 + c]

    def pair(buf, zz):
        return buf.at[:, zz * 2 + c]

    def same(mv, i, ref, device):
        return mv.copy(i, ref, ref, device)

    def w_start(i, buf):
        mv = w_mover(i)
        own = blk(buf, yl, z)
        go(same(mv, 0, own, dev_yl))
        go(same(mv, 1, own, dev_z(1)))
        go(same(mv, 6, own, dev_z(-1)))
        go(same(mv, 11, own, dev_c))

    def w_yl(i, buf):
        mv = w_mover(i)
        other = blk(buf, 1 - yl, z)
        same(mv, 0, other, dev_yl).wait_recv()
        go(same(mv, 2, other, dev_z(1)))
        go(same(mv, 7, other, dev_z(-1)))
        go(same(mv, 12, other, dev_c))

    def w_step(i, buf, k):
        mv = w_mover(i)
        for sign, base in ((-1, 1), (1, 6)):
            zz = at_z(sign * (k + 1))
            to = dev_z(-sign)
            cls = yl if sign < 0 else 1 - yl
            if k == 0:
                same(mv, base, blk(buf, yl, zz), to).wait_recv()
                same(mv, base + 1, blk(buf, 1 - yl, zz), to).wait_recv()
            elif k < 3:
                same(mv, base + 1 + k, pair(buf, zz), to).wait_recv()
            else:
                same(mv, base + 4, blk(buf, cls, zz), to).wait_recv()
            if k < 2:
                go(same(mv, base + 2 + k, pair(buf, zz), to))
            elif k == 2:
                go(same(mv, base + 4, blk(buf, cls, zz), to))
            ci = 13 + 2 * k + (0 if sign < 0 else 1)
            go(same(mv, ci, pair(buf, zz) if k < 3 else blk(buf, cls, zz), dev_c))

    def w_finish(i, buf):
        mv = w_mover(i)

        def theirs(cls, zz):
            return buf.at[cls, zz * 2 + 1 - c]

        def theirs2(zz):
            return buf.at[:, zz * 2 + 1 - c]

        same(mv, 11, theirs(yl, z), dev_c).wait_recv()
        same(mv, 12, theirs(1 - yl, z), dev_c).wait_recv()
        for k in range(4):
            for sign in (-1, 1):
                zz = at_z(sign * (k + 1))
                cls = yl if sign < 0 else 1 - yl
                ci = 13 + 2 * k + (0 if sign < 0 else 1)
                same(mv, ci, theirs2(zz) if k < 3 else theirs(cls, zz), dev_c).wait_recv()

    def rs_a(mv, part, land, a, o):
        return mv.copy(o, part.at[at_x(o), :, pl.ds(0, a)], land.at[o - 1], dev_x(o))

    def rs_b(mv, part, land, a, o):
        rows = part.shape[2]
        cc = at_x(o)
        return mv.copy(4 + o, part.at[cc, 1 - h, pl.ds(a, rows - a)], land.at[cc], dev_h)

    def rs_sends(mv, part, land_a, land_b, a, o):
        rs_b(mv, part, land_b, a, o).start()

        @pl.when(o > 0)
        def _():
            rs_a(mv, part, land_a, a, o).start()

    def rs_middle(mv, part, land_a, land_b, sum_b, land_bx, sum_a, land_ay, a):
        rows = part.shape[2]
        for o in (3, 2, 1):
            cc = at_x(o)
            rs_b(mv, part, land_b, a, o).wait_recv()
            sum_b[o - 1] = (part[cc, h, a:rows].astype(F32) + land_b[cc].astype(F32)).astype(BF)
            go(mv.copy(8 + o, sum_b.at[o - 1], land_bx.at[o - 1], dev_x(o)))
        for o in (3, 1, 2):
            rs_a(mv, part, land_a, a, o).wait_recv()
        total = part[x, 1 - h, 0:a].astype(F32)
        for o in (1, 2, 3):
            total += land_a[o - 1, 1 - h].astype(F32)
        sum_a[...] = total.astype(BF)
        go(mv.copy(8, sum_a, land_ay, dev_h))
        rs_b(mv, part, land_b, a, 0).wait_recv()

    def rs_last(mv, part, land_a, land_b, sum_b, land_bx, sum_a, land_ay, a):
        rows = part.shape[2]
        tb = part[x, h, a:rows].astype(F32) + land_b[x].astype(F32)
        for o in (1, 3, 2):
            mv.copy(8 + o, sum_b.at[o - 1], land_bx.at[o - 1], dev_x(o)).wait_recv()
            tb += land_bx[o - 1].astype(F32)
        ta = part[x, h, 0:a].astype(F32)
        for o in (1, 2, 3):
            ta += land_a[o - 1, h].astype(F32)
        mv.copy(8, sum_a, land_ay, dev_h).wait_recv()
        ta += land_ay[...].astype(F32)
        return ta, tb

    def rs_sent(mv, part, land_a, land_b, a):
        for o in range(4):
            rs_b(mv, part, land_b, a, o).wait_send()
            if o:
                rs_a(mv, part, land_a, a, o).wait_send()

    c_hid.wait()
    ag_start(hm, hbuf)
    c_wq.wait()
    w_start(0, wqb)
    c_w1.wait()
    c_w2.wait()

    rm, bm = Mover(rs, rr), Mover(bs, br)

    def enc_chunk(i, carry):
        o = 3 - i
        cc = at_x(o)
        c_nb(o).wait()
        v = nbv[cc].astype(F32)
        scale = lax.rsqrt(jnp.mean(v * v, axis=-1, keepdims=True) + 1e-06)
        norm = (v * scale * eg[...]).astype(BF)
        inner = jnp.maximum(dot_t(norm, w1v[...]), 0.0).astype(BF)
        pbuf[cc] = dot(inner, w2v[...]).astype(BF).reshape(2, 128, 896)
        rs_sends(rm, pbuf, ra, ryb, ENC_A, o)
        return carry

    lax.fori_loop(0, NX, enc_chunk, 0)

    w_yl(0, wqb)
    c_wo.wait()
    ag_pass_a(hm, hbuf, DEC_A)
    w_step(0, wqb, 0)
    w_start(1, wob)
    for k in (1, 3, 2):
        ag_pass_b(hm, hbuf, DEC_A, k)
    enc_rs = (rm, pbuf, ra, ryb, sb, rbx, sa, ray, ENC_A)
    rs_middle(*enc_rs)
    w_step(0, wqb, 1)
    w_yl(1, wob)
    ta, tb = rs_last(*enc_rs)
    ebuf[x, h, 0:ENC_A] = (nbv[x, pl.ds(pl.multiple_of(h * 128, 128), ENC_A)].astype(F32) + ta).astype(BF)
    ebuf[x, h, ENC_A:128] = (
        nbv[x, pl.ds(pl.multiple_of(h * 128 + ENC_A, 16), 128 - ENC_A)].astype(F32) + tb
    ).astype(BF)
    ag_start(em, ebuf)
    w_step(0, wqb, 2)
    w_step(1, wob, 0)
    w_step(0, wqb, 3)
    ag_pass_a(em, ebuf, ENC_A)
    for k in (1, 2, 3):
        ag_a_in(hm, hbuf, DEC_A, k).wait_recv()
        ag_b_in(hm, hbuf, DEC_A, k).wait_recv()
    w_finish(0, wqb)

    total = jnp.zeros((256, 1), F32)
    for i in range(8):
        v = hbuf[i // 2, i % 2].astype(F32)
        total += jnp.sum(v * v, axis=-1, keepdims=True)
    scale = lax.rsqrt(total * (1.0 / 4096.0) + 1e-06)
    acc[...] = jnp.zeros_like(acc)

    def query_block(i, carry):
        v = hbuf[lax.div(i, 2), lax.rem(i, 2)].astype(F32)
        norm = (v * scale * dg[i]).astype(BF)
        w = wqb[lax.div(i, 4), pl.ds(lax.rem(i, 4) * 4, 4)].reshape(512, 512)
        acc[...] += dot(norm, w)
        return carry

    lax.fori_loop(0, 8, query_block, 0)
    qv[...] = acc[...].astype(BF)
    xm = Mover(xs, xr)
    q_halo = xm.copy(0, qv.at[pl.ds(0, M)], qn, dev_prev)
    go(q_halo)
    w_step(1, wob, 1)
    for k in (1, 3, 2):
        ag_pass_b(em, ebuf, ENC_A, k)
    q_halo.wait_recv()
    joined = jnp.concatenate([qv[...].astype(F32), qn[...].astype(F32)], axis=0)
    qs[...] = pltpu.roll(joined, 1, 0)[M : M + 256].astype(BF)
    c_wk.wait()
    c_wv.wait()

    a_halo = xm.copy(1, at.at[pl.ds(3 * M, M)], an, dev_next)

    def span(o, carry):
        cc = at_x(NX - o)

        @pl.when(o > 0)
        def _():
            ag_a_in(em, ebuf, ENC_A, o).wait_recv()
            ag_b_in(em, ebuf, ENC_A, o).wait_recv()

        e = ebuf[cc].reshape(256, 896)
        keys = dot(e, wkv[...]).astype(BF)
        values = dot(e, wvv[...]).astype(BF)
        rows = pl.ds(pl.multiple_of(cc * M, M), M)
        q = qs[rows]
        for j in range(4):
            cols = slice(j * HD, (j + 1) * HD)
            scores = dot_t(q[:, cols], keys[:, cols]) * HD ** (-0.5)
            ex = jnp.exp(scores - jnp.max(scores, axis=-1, keepdims=True))
            probs = (ex / jnp.sum(ex, axis=-1, keepdims=True)).astype(BF)
            at[rows, cols] = dot(probs, values[:, cols]).astype(BF)

        @pl.when(cc == 3)
        def _():
            a_halo.start()

        return carry

    lax.fori_loop(0, NX, span, 0)
    w_step(1, wob, 2)
    w_step(1, wob, 3)
    a_halo.wait_recv()
    joined = jnp.concatenate([an[...].astype(F32), at[0:200].astype(F32)], axis=0)
    mine = pltpu.roll(joined, 263, 0)[0:256]
    position = s * 256 + lax.broadcasted_iota(jnp.int32, (256, 512), 0)
    af[...] = jnp.where(position >= M - 1, mine, 0.0).astype(BF)
    w_finish(1, wob)

    def out_block(i, carry):
        o = 3 - i
        cc = at_x(o)
        for hh in range(2):
            tt = cc * 2 + hh
            first = lax.rem(tt, 4) * 4
            w = jnp.concatenate([wob[lax.div(tt, 4), first + n] for n in range(4)], axis=1)
            obuf[cc, hh] = dot(af[...], w).astype(BF)
        rs_sends(bm, obuf, oa, oyb, DEC_A, o)
        return carry

    lax.fori_loop(0, NX, out_block, 0)
    dec_rs = (bm, obuf, oa, oyb, osb, obx, osa, oay, DEC_A)
    rs_middle(*dec_rs)
    ta, tb = rs_last(*dec_rs)
    out[0:DEC_A] = (hbuf[x, h, 0:DEC_A].astype(F32) + ta).astype(BF)
    out[DEC_A:256] = (hbuf[x, h, DEC_A:256].astype(F32) + tb).astype(BF)

    for cp in started:
        cp.wait_send()
    a_halo.wait_send()
    rs_sent(rm, pbuf, ra, ryb, ENC_A)
    rs_sent(bm, obuf, oa, oyb, DEC_A)


def per_device(hidden, neighbours, enc_gain, enc_w1, enc_w2, key_weight, value_weight, dec_gain, query_weight, out_weight):
    dma = pltpu.SemaphoreType.DMA
    ea, eb, da, db = ENC_A, 128 - ENC_A, DEC_A, 256 - DEC_A
    V = pltpu.VMEM
    any_ = pl.BlockSpec(memory_space=pl.ANY)
    vm = pl.BlockSpec(memory_space=pltpu.VMEM)
    return pl.pallas_call(
        kernel,
        out_shape=jax.ShapeDtypeStruct((256, 512), BF),
        in_specs=[any_, any_, vm, any_, any_, any_, any_, vm, any_, any_],
        out_specs=vm,
        scratch_shapes=[
            V((4, 256, 896), BF), V((448, 896), BF), V((448, 896), BF), V((896, 512), BF), V((896, 512), BF),
            V((4, 2, 256, 512), BF), V((2, 16, 128, 512), BF), V((2, 16, 512, 128), BF),
            V((4, 2, 128, 896), BF), V((3, 2, ea, 896), BF), V((4, eb, 896), BF), V((3, eb, 896), BF),
            V((3, eb, 896), BF), V((ea, 896), BF), V((ea, 896), BF), V((4, 2, 128, 896), BF),
            V((256, 512), F32), V((256, 512), BF), V((64, 512), BF), V((256, 512), BF), V((256, 512), BF),
            V((64, 512), BF), V((256, 512), BF),
            V((4, 2, 256, 512), BF), V((3, 2, da, 512), BF), V((4, db, 512), BF), V((3, db, 512), BF),
            V((3, db, 512), BF), V((da, 512), BF), V((da, 512), BF),
            dma((11,)), dma((10,)), dma((10,)), dma((10,)), dma((10,)), dma((12,)), dma((12,)), dma((12,)), dma((12,)),
            dma((2, 21)), dma((2, 21)), dma((2,)), dma((2,)),
        ],
        compiler_params=pltpu.CompilerParams(collective_id=0, has_side_effects=True, vmem_limit_bytes=60 * 1024 * 1024),
        name="layer",
    )(
        hidden, neighbours, enc_gain.reshape(1, -1), enc_w1.T, enc_w2, key_weight, value_weight,
        dec_gain.reshape(8, 1, 512), query_weight, out_weight,
    )


def solution(mesh):
    placed = (
        P("seq", "tp"), P("seq", None, None), P(), P(None, "tp"), P("tp", None), P(None, "tp"), P(None, "tp"), P(),
        P("seq", "tp"), P("tp", "seq"),
    )
    return jax.shard_map(per_device, mesh=mesh, in_specs=placed, out_specs=P("seq", "tp"), check_vma=False)
```

```python
import functools

import jax
import jax.numpy as jnp
from jax import lax
from jax.experimental import pallas as pl
from jax.experimental.pallas import tpu as pltpu
from jax.sharding import PartitionSpec as P

HD = 128
M = 64
BF = jnp.bfloat16
F32 = jnp.float32
MESH = pl.DeviceIdType.MESH

NX = 4
NZ = 8
ENC_A = 64
DEC_A = 128


def dot(a, b):
    return jnp.dot(a, b, preferred_element_type=F32)


def dot_t(a, b):
    return lax.dot_general(a, b, (((1,), (1,)), ((), ())), preferred_element_type=F32)


class Mover:
    def __init__(self, send, recv):
        self.send, self.recv = send, recv

    def copy(self, i, src, dst, device):
        return pltpu.make_async_remote_copy(
            src_ref=src,
            dst_ref=dst,
            send_sem=self.send.at[i],
            recv_sem=self.recv.at[i],
            device_id=device,
            device_id_type=MESH,
        )


def kernel(
    hid, nb, eg, w1, w2, wk, wv, dg, wq, wo, out,
    nbv, w1v, w2v, wkv, wvv, hbuf, wqb, wob,
    pbuf, ra, ryb, sb, rbx, sa, ray, ebuf,
    acc, qv, qn, qs, at, an, af,
    obuf, oin, own,
    lsem, hs, hr, es, er, rs, rr, bs, br, ws, wr, xs, xr,
):
    s = lax.axis_index("seq")
    t = lax.axis_index("tp")
    x, h = lax.div(t, 2), lax.rem(t, 2)
    yl, zc = lax.div(s, 16), lax.rem(s, 16)
    z, c = lax.div(zc, 2), lax.rem(zc, 2)
    nseq = lax.axis_size("seq")

    def at_x(k):
        return lax.rem(x + k, NX)

    def dev_x(k):
        return (s, at_x(k) * 2 + h)

    dev_h = (s, x * 2 + 1 - h)

    def active(zz):
        return lax.rem(lax.div(zz, 2), 2) == h

    def slot(zz):
        return lax.div(zz, 4) * 2 + lax.rem(zz, 2)

    def at_z(k):
        return lax.rem(z + k + NZ, NZ)

    def dev_z(k):
        return (yl * 16 + at_z(k) * 2 + c, t)

    dev_c = (yl * 16 + z * 2 + 1 - c, t)
    dev_yl = ((1 - yl) * 16 + zc, t)
    dev_next = (lax.rem(s + 1, nseq), t)
    dev_prev = (lax.rem(s + nseq - 1, nseq), t)
    dev_next_h = (lax.rem(s + 1, nseq), x * 2 + 1 - h)
    dev_prev_h = (lax.rem(s + nseq - 1, nseq), x * 2 + 1 - h)

    def local(i, src, dst):
        return pltpu.make_async_copy(src, dst, lsem.at[i])

    c_hid = local(0, hid, hbuf.at[x, h])
    c_wq = local(1, wq, wqb.at[yl, zc])
    c_w1 = local(2, w1, w1v)
    c_w2 = local(3, w2, w2v)
    c_wo = local(4, wo, wob.at[yl, slot(z), c, h])
    c_wk = local(5, wk, wkv)
    c_wv = local(6, wv, wvv)

    def c_nb(o):
        return local(7 + o, nb.at[at_x(o)], nbv.at[at_x(o)])

    c_hid.start()
    c_wq.start()
    c_nb(3).start()
    c_w1.start()
    c_w2.start()
    c_nb(2).start()
    c_nb(1).start()
    c_nb(0).start()

    @pl.when(active(z))
    def _():
        c_wo.start()

    c_wk.start()
    c_wv.start()

    barrier = pltpu.get_barrier_semaphore()
    partners = [dev_x(1), dev_x(2), dev_x(3), dev_h, dev_z(1), dev_z(-1), dev_c, dev_yl, dev_next, dev_prev, dev_next_h, dev_prev_h]
    for device in partners:
        pl.semaphore_signal(barrier, inc=1, device_id=device, device_id_type=MESH)
    pl.semaphore_wait(barrier, len(partners))

    started = []

    def go(cp, cond=None):
        if cond is None:
            cp.start()
        else:
            pl.when(cond)(cp.start)
        started.append((cp, cond))

    class Gather:
        def __init__(self, mv, buf, first):
            self.mv, self.buf, self.a, self.b = mv, buf, first, buf.shape[2] - first

        def at(self, i, cc, hh, top, device):
            ref = self.buf.at[cc, hh, pl.ds(0, self.a) if top else pl.ds(self.a, self.b)]
            return self.mv.copy(i, ref, ref, device)

        def first_a(self):
            go(self.at(0, x, h, True, dev_h))

        def first_b(self):
            for k in (2, 1, 3):
                go(self.at(k, x, h, False, dev_x(k)))

        def own_a(self):
            for k in (2, 1, 3):
                go(self.at(3 + k, x, h, True, dev_x(k)))

        def own_b(self):
            go(self.at(7, x, h, False, dev_h))

        def pass_a(self):
            self.at(0, x, 1 - h, True, dev_h).wait_recv()
            for k in (2, 1, 3):
                go(self.at(7 + k, x, 1 - h, True, dev_x(k)))

        def pass_b(self, k):
            self.at(k, at_x(NX - k), h, False, dev_h).wait_recv()
            go(self.at(10 + k, at_x(NX - k), h, False, dev_h))

        def near(self):
            self.at(7, x, 1 - h, False, dev_h).wait_recv()

        def rest(self, k):
            cc = at_x(NX - k)
            self.at(3 + k, cc, h, True, dev_h).wait_recv()
            self.at(7 + k, cc, 1 - h, True, dev_h).wait_recv()
            self.at(10 + k, cc, 1 - h, False, dev_h).wait_recv()

    def when(cond, f):
        if cond is None:
            f()
        else:
            pl.when(cond)(f)

    class Ring:
        def __init__(self, i, unit, here):
            self.mv, self.unit, self.here = Mover(ws.at[i], wr.at[i]), unit, here

        def same(self, i, ref, device):
            return self.mv.copy(i, ref, ref, device)

        def start(self):
            own, on = self.unit(yl, z, c), self.here(z)
            go(self.same(0, own, dev_yl), on)
            go(self.same(1, own, dev_z(1)), on)
            go(self.same(8, own, dev_z(-1)), on)
            go(self.same(15, own, dev_c), on)

        def across(self):
            other, on = self.unit(1 - yl, z, c), self.here(z)
            when(on, self.same(0, other, dev_yl).wait_recv)
            go(self.same(2, other, dev_z(1)), on)
            go(self.same(9, other, dev_z(-1)), on)
            go(self.same(16, other, dev_c), on)

        def step(self, k, other):
            for d, sign in enumerate((-1, 1)):
                if k == 3 and other != d:
                    continue
                zz = at_z(sign * (k + 1))
                to, on = dev_z(-sign), self.here(zz)
                ref = self.unit(1 - yl if other else yl, zz, c)
                i = 1 + 7 * d + (6 if k == 3 else 2 * k + other)
                when(on, self.same(i, ref, to).wait_recv)
                if k < 2 or (k == 2 and other == d):
                    go(self.same(1 + 7 * d + (6 if k == 2 else 2 * k + 2 + other), ref, to), on)
                go(self.same(17 + 4 * k + (d if k == 3 else 2 * d + other), ref, dev_c), on)

        def finish(self):
            def wait(i, cls, zz):
                when(self.here(zz), self.same(i, self.unit(cls, zz, 1 - c), dev_c).wait_recv)

            wait(15, yl, z)
            wait(16, 1 - yl, z)
            for k in range(4):
                for d, sign in enumerate((-1, 1)):
                    for other in range(2):
                        if k == 3 and other != d:
                            continue
                        i = 17 + 4 * k + (d if k == 3 else 2 * d + other)
                        wait(i, 1 - yl if other else yl, at_z(sign * (k + 1)))

    def rs_a(mv, part, land, a, o):
        return mv.copy(o, part.at[at_x(o), :, pl.ds(0, a)], land.at[o - 1], dev_x(o))

    def rs_b(mv, part, land, a, o):
        rows = part.shape[2]
        cc = at_x(o)
        return mv.copy(4 + o, part.at[cc, 1 - h, pl.ds(a, rows - a)], land.at[cc], dev_h)

    def rs_sends(mv, part, land_a, land_b, a, o):
        rs_b(mv, part, land_b, a, o).start()

        @pl.when(o > 0)
        def _():
            rs_a(mv, part, land_a, a, o).start()

    def rs_middle(mv, part, land_a, land_b, sum_b, land_bx, sum_a, land_ay, a):
        rows = part.shape[2]
        for o in (3, 2, 1):
            cc = at_x(o)
            rs_b(mv, part, land_b, a, o).wait_recv()
            sum_b[o - 1] = (part[cc, h, a:rows].astype(F32) + land_b[cc].astype(F32)).astype(BF)
            go(mv.copy(8 + o, sum_b.at[o - 1], land_bx.at[o - 1], dev_x(o)))
        for o in (3, 1, 2):
            rs_a(mv, part, land_a, a, o).wait_recv()
        total = part[x, 1 - h, 0:a].astype(F32)
        for o in (1, 2, 3):
            total += land_a[o - 1, 1 - h].astype(F32)
        sum_a[...] = total.astype(BF)
        go(mv.copy(8, sum_a, land_ay, dev_h))
        rs_b(mv, part, land_b, a, 0).wait_recv()

    def rs_last(mv, part, land_a, land_b, sum_b, land_bx, sum_a, land_ay, a):
        rows = part.shape[2]
        tb = part[x, h, a:rows].astype(F32) + land_b[x].astype(F32)
        for o in (1, 3, 2):
            mv.copy(8 + o, sum_b.at[o - 1], land_bx.at[o - 1], dev_x(o)).wait_recv()
            tb += land_bx[o - 1].astype(F32)
        ta = part[x, h, 0:a].astype(F32)
        for o in (1, 2, 3):
            ta += land_a[o - 1, h].astype(F32)
        mv.copy(8, sum_a, land_ay, dev_h).wait_recv()
        ta += land_ay[...].astype(F32)
        return ta, tb

    def rs_sent(mv, part, land_a, land_b, a):
        for o in range(4):
            rs_b(mv, part, land_b, a, o).wait_send()
            if o:
                rs_a(mv, part, land_a, a, o).wait_send()

    rm, bm, xm = Mover(rs, rr), Mover(bs, br), Mover(xs, xr)
    gd, ge = Gather(Mover(hs, hr), hbuf, DEC_A), Gather(Mover(es, er), ebuf, ENC_A)
    rq = Ring(0, lambda cls, zz, core: wqb.at[cls, zz * 2 + core], lambda zz: None)
    ro = Ring(1, lambda cls, zz, core: wob.at[cls, slot(zz), core], active)

    c_wq.wait()
    rq.start()
    theirs = wob.at[yl, slot(z), c, h]
    go(ro.mv.copy(31, wo, theirs, dev_h), jnp.logical_not(active(z)))
    c_hid.wait()
    gd.first_a()
    gd.first_b()
    c_w1.wait()
    c_w2.wait()

    def enc_chunk(i, carry):
        o = 3 - i
        cc = at_x(o)
        c_nb(o).wait()
        v = nbv[cc].astype(F32)
        scale = lax.rsqrt(jnp.mean(v * v, axis=-1, keepdims=True) + 1e-06)
        norm = (v * scale * eg[...].reshape(1, 896)).astype(BF)
        inner = jnp.maximum(dot_t(norm, w1v[...]), 0.0).astype(BF)
        pbuf[cc] = dot(inner, w2v[...]).astype(BF).reshape(2, 128, 896)
        rs_sends(rm, pbuf, ra, ryb, ENC_A, o)
        return carry

    lax.fori_loop(0, NX, enc_chunk, 0)

    rq.across()

    @pl.when(active(z))
    def _():
        c_wo.wait()
        handed = wob.at[yl, slot(z), c, 1 - h]
        ro.mv.copy(31, handed, handed, dev_h).wait_recv()

    ro.start()
    gd.own_a()
    gd.own_b()
    rq.step(0, 0)
    rq.step(0, 1)
    rq.step(1, 0)
    rq.step(1, 1)
    enc_rs = (rm, pbuf, ra, ryb, sb, rbx, sa, ray, ENC_A)
    rs_middle(*enc_rs)
    gd.pass_a()
    for k in (1, 3, 2):
        gd.pass_b(k)
    ro.step(0, 0)
    rq.step(2, 0)
    rq.step(2, 1)
    ro.across()
    ta, tb = rs_last(*enc_rs)
    ebuf[x, h, 0:ENC_A] = (nbv[x, pl.ds(pl.multiple_of(h * 128, 128), ENC_A)].astype(F32) + ta).astype(BF)
    ge.first_a()
    ebuf[x, h, ENC_A:128] = (
        nbv[x, pl.ds(pl.multiple_of(h * 128 + ENC_A, 16), 128 - ENC_A)].astype(F32) + tb
    ).astype(BF)
    ge.first_b()
    ge.own_a()
    ge.own_b()
    rq.step(3, 0)
    rq.step(3, 1)
    ro.step(1, 0)
    ge.pass_a()
    ro.step(0, 1)
    gd.near()
    for k in (1, 3, 2):
        gd.rest(k)
    rq.finish()

    total = jnp.zeros((256, 1), F32)
    for i in range(8):
        v = hbuf[i // 2, i % 2].astype(F32)
        total += jnp.sum(v * v, axis=-1, keepdims=True)
    scale = lax.rsqrt(total * (1.0 / 4096.0) + 1e-06)
    acc[...] = jnp.zeros_like(acc)

    def query_block(i, carry):
        v = hbuf[lax.div(i, 2), lax.rem(i, 2)].astype(F32)
        norm = (v * scale * dg[i]).astype(BF)
        w = wqb[lax.div(i, 4), pl.ds(lax.rem(i, 4) * 4, 4)].reshape(512, 512)
        acc[...] += dot(norm, w)
        return carry

    lax.fori_loop(0, 8, query_block, 0)
    qv[...] = acc[...].astype(BF)
    q_halo = xm.copy(0, qv.at[pl.ds(0, M)], qn, dev_prev)
    go(q_halo)
    for k in (1, 3, 2):
        ge.pass_b(k)
    ro.step(2, 0)
    ro.step(1, 1)
    c_wk.wait()
    c_wv.wait()
    q_halo.wait_recv()
    joined = jnp.concatenate([qv[...].astype(F32), qn[...].astype(F32)], axis=0)
    qs[...] = pltpu.roll(joined, 1, 0)[M : M + 256].astype(BF)

    def at_copy(cc):
        rows = pl.ds(pl.multiple_of(cc * M, M), M)
        return xm.copy(4 + cc, at.at[h, rows], at.at[h, rows], dev_h)

    def at_copy_in(cc):
        rows = pl.ds(pl.multiple_of(cc * M, M), M)
        return xm.copy(4 + cc, at.at[1 - h, rows], at.at[1 - h, rows], dev_h)

    a_halo = xm.copy(1, at.at[h, pl.ds(3 * M, M)], an.at[h], dev_next)
    a_halo_h = xm.copy(8, at.at[h, pl.ds(3 * M, M)], an.at[h], dev_next_h)

    def span(o, carry):
        cc = at_x(NX - o)

        @pl.when(o > 0)
        def _():
            ge.rest(o)

        @pl.when(o == 0)
        def _():
            ge.near()

        e = ebuf[cc].reshape(256, 896)
        keys = dot(e, wkv[...]).astype(BF)
        values = dot(e, wvv[...]).astype(BF)
        rows = pl.ds(pl.multiple_of(cc * M, M), M)
        q = qs[rows]
        for j in range(4):
            cols = slice(j * HD, (j + 1) * HD)
            scores = dot_t(q[:, cols], keys[:, cols]) * HD ** (-0.5)
            ex = jnp.exp(scores - jnp.max(scores, axis=-1, keepdims=True))
            probs = (ex / jnp.sum(ex, axis=-1, keepdims=True)).astype(BF)
            at[h, rows, cols] = dot(probs, values[:, cols]).astype(BF)

        @pl.when(cc == 3)
        def _():
            a_halo.start()
            a_halo_h.start()

        at_copy(cc).start()
        return carry

    lax.fori_loop(0, NX, span, 0)
    ro.step(3, 0)
    ro.step(2, 1)
    ro.step(3, 1)
    ro.finish()
    a_halo.wait_recv()
    xm.copy(8, an.at[1 - h], an.at[1 - h], dev_h).wait_recv()
    for cc in range(4):
        at_copy_in(cc).wait_recv()
    position = s * 256 + lax.broadcasted_iota(jnp.int32, (256, 512), 0)
    for hh in range(2):
        joined = jnp.concatenate([an[hh].astype(F32), at[hh, 0:200].astype(F32)], axis=0)
        mine = pltpu.roll(joined, 263, 0)[0:256]
        af[hh] = jnp.where(position >= M - 1, mine, 0.0).astype(BF)

    def o_copy(o):
        return bm.copy(o - 1, obuf.at[o - 1], oin.at[o - 1], dev_x(o))

    def out_block(i, carry):
        o = jnp.where(i == 0, 2, jnp.where(i == 1, 1, jnp.where(i == 2, 3, 0)))
        cc = at_x(o)
        part = jnp.zeros((256, 512), F32)
        for hh in range(2):
            first = lax.rem(cc, 2) * 2
            w = [wob[lax.div(cc, 2), first + n // 2, n % 2, hh] for n in range(4)]
            part += dot(af[hh], jnp.concatenate(w, axis=1))

        @pl.when(o > 0)
        def _():
            obuf[o - 1] = part.astype(BF)
            o_copy(o).start()

        @pl.when(o == 0)
        def _():
            own[...] = hbuf[x, h].astype(F32) + part

        return carry

    lax.fori_loop(0, NX, out_block, 0)
    for o in (1, 3, 2):
        o_copy(o).wait_recv()
    out[...] = (own[...] + oin[0].astype(F32) + oin[1].astype(F32) + oin[2].astype(F32)).astype(BF)

    for cp, cond in started:
        if cond is None:
            cp.wait_send()
        else:
            pl.when(cond)(cp.wait_send)
    a_halo.wait_send()
    a_halo_h.wait_send()
    for k in range(4):
        at_copy(k).wait_send()
        if k:
            o_copy(k).wait_send()
    rs_sent(rm, pbuf, ra, ryb, ENC_A)


def per_device(hidden, neighbours, enc_gain, enc_w1, enc_w2, key_weight, value_weight, dec_gain, query_weight, out_weight):
    dma = pltpu.SemaphoreType.DMA
    ea, eb = ENC_A, 128 - ENC_A
    V = pltpu.VMEM
    any_ = pl.BlockSpec(memory_space=pl.ANY)
    vm = pl.BlockSpec(memory_space=pltpu.VMEM)
    return pl.pallas_call(
        kernel,
        out_shape=jax.ShapeDtypeStruct((256, 512), BF),
        in_specs=[any_, any_, vm, any_, any_, any_, any_, vm, any_, any_],
        out_specs=vm,
        scratch_shapes=[
            V((4, 256, 896), BF), V((448, 896), BF), V((448, 896), BF), V((896, 512), BF), V((896, 512), BF),
            V((4, 2, 256, 512), BF), V((2, 16, 128, 512), BF), V((2, 4, 2, 2, 512, 128), BF),
            V((4, 2, 128, 896), BF), V((3, 2, ea, 896), BF), V((4, eb, 896), BF), V((3, eb, 896), BF),
            V((3, eb, 896), BF), V((ea, 896), BF), V((ea, 896), BF), V((4, 2, 128, 896), BF),
            V((256, 512), F32), V((256, 512), BF), V((64, 512), BF), V((256, 512), BF), V((2, 256, 512), BF),
            V((2, 64, 512), BF), V((2, 256, 512), BF),
            V((3, 256, 512), BF), V((3, 256, 512), BF), V((256, 512), F32),
            dma((11,)), dma((14,)), dma((14,)), dma((14,)), dma((14,)), dma((12,)), dma((12,)), dma((3,)), dma((3,)),
            dma((2, 32)), dma((2, 32)), dma((9,)), dma((9,)),
        ],
        compiler_params=pltpu.CompilerParams(collective_id=0, has_side_effects=True, vmem_limit_bytes=60 * 1024 * 1024),
        name="layer",
    )(
        hidden, neighbours, enc_gain, enc_w1.T, enc_w2, key_weight, value_weight,
        dec_gain.reshape(8, 1, 512), query_weight, out_weight,
    )


def solution(mesh):
    placed = (
        P("seq", "tp"), P("seq", None, None), P(), P(None, "tp"), P("tp", None), P(None, "tp"), P(None, "tp"), P(),
        P("seq", "tp"), P("tp", "seq"),
    )
    return jax.shard_map(per_device, mesh=mesh, in_specs=placed, out_specs=P("seq", "tp"), check_vma=False)
```
